256 devices in a mesh: frame: 64 (over z, x, core), chan: 4 (over y).
Axes of the slice: x: 4, y: 4, z: 8, core: 2. Of those that a mesh axis runs over, the one named last changes fastest.
Arguments:
- query_act: bfloat16 [56320, 2240], P('frame', 'chan'), may hold values from -6 to 6
- key_act: bfloat16 [56320, 2240], P('frame', 'chan'), may hold values from -6 to 6
- value_act: bfloat16 [56320, 2240], P('frame', 'chan'), may hold values from -6 to 6
- conv_weight: bfloat16 [3, 2240, 2240], P(None, 'chan'), may hold values from -0.109375 to 0.109375
- gate_act: bfloat16 [56320, 2240], P('frame', 'chan'), may hold values from -8 to 8
Outputs:
- layer_out: bfloat16 [56320, 2240], P('frame', 'chan')
The draws below stay inside these ranges and needn't reach their ends.
All inputs are finite; a program needn't handle non-finite values.
Results may differ from the reference program's by a relative error of at most 0.015.
Values may be sent and summed in bfloat16 or wider, within the bound.
No kernel may reach another device: no remote copies, remote signals or barrier semaphores. Data moves between devices by JAX's collectives and lax.ppermute only.
A program may use at most 128 MiB of HBM per device.

```python
import jax
import jax.numpy as jnp
from jax import lax

D = 2240
HEADS = 20
HD = 112
TPF = 880
TOKENS = 56320
N_CHAN = 4


def raised(array, key, source, target, shards_of, factor):
    owner, partner = [(jnp.arange(array.shape[axis_at]) // (array.shape[axis_at] // shards_of)).reshape([-1 if axis == axis_at else 1 for axis in range(array.ndim)]) for axis_at in (source, target)]
    chosen = jax.random.permutation(key, shards_of)[partner]
    strong = (owner == chosen) | (owner == (partner + shards_of // 2) % shards_of)
    return jnp.where(strong, factor * array, array)


def block_levels(rng, extent, pieces, smallest, largest):
    factor_of, own = 1.0, jax.random.fold_in(rng, 6)
    for position, parts in pieces:
        draws = jnp.exp(jax.random.uniform(jax.random.fold_in(own, position), (parts,), jnp.float32, smallest / len(pieces), largest / len(pieces)))
        factor_of = factor_of * jnp.repeat(draws, extent[position] // parts).reshape([-1 if axis == position else 1 for axis in range(len(extent))])
    return factor_of


def noise(own_key, extent, width, limit, cuts=(), kind=jnp.bfloat16):
    result = width * jax.random.normal(own_key, extent, jnp.float32)
    if cuts:
        result = result * block_levels(own_key, extent, cuts, -0.22, 0.18)
    return jnp.clip(result, -limit, limit).astype(kind)


def gaussian_with(stream_key, shape, scale, most, pieces, heavy, dtype=jnp.bfloat16):
    drawn = scale * jax.random.normal(stream_key, shape, jnp.float32)
    if pieces:
        drawn = drawn * block_levels(stream_key, shape, pieces, -0.22, 0.18)
    return jnp.clip(raised(drawn, jax.random.fold_in(stream_key, 3), *heavy), -most, most).astype(dtype)


def setup_inputs(seed: int = 0) -> dict:
    splits = jax.random.split(jax.random.key(seed), 6)
    return {
        "query_act": noise(splits[0], (TOKENS, D), 1.0, 6.0, ((0, 64), (1, 4))),
        "key_act": noise(splits[1], (TOKENS, D), 1.0, 6.0, ((0, 64), (1, 4))),
        "value_act": noise(splits[2], (TOKENS, D), 1.0, 6.0, ((0, 64), (1, 4))),
        "conv_weight": gaussian_with(splits[3], (3, D, D), (3 * D) ** -0.5, 0.109375, ((1, 4),), (1, 2, 4, 2.0)),
        "gate_act": noise(splits[4], (TOKENS, D), 1.5, 8.0, ((0, 64), (1, 4))),
    }


def reference(query_act, key_act, value_act, conv_weight, gate_act):
    frame_count = TOKENS // TPF
    key_feat = jnp.maximum(key_act, 0).astype(jnp.float32).reshape(frame_count, TPF, HEADS, HD)
    value_feat = value_act.astype(jnp.float32).reshape(frame_count, TPF, HEADS, HD)
    query_feat = jnp.maximum(query_act, 0).astype(jnp.float32).reshape(frame_count, TPF, HEADS, HD)
    frame_state = jnp.einsum('ftha,fthb->fhab', key_feat, value_feat)
    prefix_state = jnp.cumsum(frame_state, axis=0).astype(jnp.bfloat16)
    prefix_state = lax.optimization_barrier(prefix_state).astype(jnp.float32)
    readout = jnp.einsum('ftha,fhab->fthb', query_feat, prefix_state)
    scale_inv = lax.rsqrt(lax.optimization_barrier(jnp.mean(readout * readout, axis=-1, keepdims=True)) + 1e-06)
    attended = (readout * scale_inv).astype(jnp.bfloat16).reshape(frame_count, TPF, D)
    with_rims = jnp.pad(attended, ((1, 1), (0, 0), (0, 0)))
    group_width = D // N_CHAN
    conv_out = jnp.zeros((frame_count * TPF, D), jnp.float32)
    for chan_group in range(N_CHAN):
        low_col = chan_group * group_width
        partials = jnp.zeros((frame_count * TPF, D), jnp.float32)
        for tap_index in range(3):
            source = with_rims[tap_index:tap_index + frame_count, :, low_col:low_col + group_width]
            partials = partials + jnp.dot(source.reshape(frame_count * TPF, group_width), conv_weight[tap_index, low_col:low_col + group_width, :], preferred_element_type=jnp.float32)
        rounded = lax.optimization_barrier(partials.astype(jnp.bfloat16))
        conv_out = conv_out + rounded.astype(jnp.float32)
    gate_value = jax.nn.silu(gate_act.astype(jnp.float32))
    return (conv_out * gate_value).astype(jnp.bfloat16)
```

```python
import jax
import jax.numpy as jnp
from jax import lax
from jax.sharding import Mesh, PartitionSpec as P

HD = 112
TPF = 880
BF = jnp.bfloat16
F32 = jnp.float32
NZ, NX, NC, NY = 8, 4, 2, 4
FR = ("z", "x", "c")


def shift(value, axis, step):
    count = lax.axis_size(axis)
    return lax.ppermute(value, axis, [(i, i + step) for i in range(count) if 0 <= i + step < count])


def ring(value, axis, step):
    count = lax.axis_size(axis)
    return lax.ppermute(value, axis, [(i, (i + step) % count) for i in range(count)])


def earlier_frames(state):
    half = state.shape[0] // 2
    core = lax.axis_index("c")
    x_at = lax.axis_index("x")
    mine = lax.dynamic_slice_in_dim(state, core * half, half, 0)
    other = lax.dynamic_slice_in_dim(state, (1 - core) * half, half, 0)
    theirs = lax.ppermute(other.astype(BF), "c", [(0, 1), (1, 0)]).astype(F32)
    chip = mine + theirs
    chip_bf = chip.astype(BF)
    total, before = chip, jnp.zeros_like(chip)
    for step in (1, 2, 3):
        got = ring(chip_bf, "x", step).astype(F32)
        total = total + got
        before = before + jnp.where(x_at >= step, got, 0.0)
    total_bf = total.astype(BF)
    one = shift(total_bf, "z", 1).astype(F32)
    two = shift(total_bf, "z", 2).astype(F32)
    near = one + two
    window = (total + near).astype(BF)
    three = shift(window, "z", 3).astype(F32)
    six = shift(window, "z", 6).astype(F32)
    before = before + (near + (three + six))
    to_other = jnp.where(core == 0, before + mine, before)
    to_self = jnp.where(core == 0, before, before + theirs)
    from_other = lax.ppermute(to_other.astype(BF), "c", [(0, 1), (1, 0)]).astype(F32)
    first = jnp.where(core == 0, to_self, from_other)
    second = jnp.where(core == 0, from_other, to_self)
    return jnp.concatenate([first, second], axis=0)


def attend(query, prefix):
    readout = jnp.einsum("hab,hat->hbt", prefix, jnp.maximum(query, 0), preferred_element_type=F32)
    scale = lax.rsqrt(jnp.mean(readout * readout, axis=1, keepdims=True) + 1e-06)
    return (readout * scale).astype(BF).reshape(-1, query.shape[-1])


def shards(query_act, key_act, value_act, conv_weight, gate_act):
    heads = query_act.shape[1] // HD
    width = heads * HD
    turned = lambda a: a.T.reshape(heads, HD, TPF)
    query = turned(query_act)
    q_prev = shift(query, FR, 1)
    q_next = shift(query, FR, -1)
    key = jnp.maximum(turned(key_act), 0)
    state = jnp.einsum("hat,hbt->hab", key, turned(value_act), preferred_element_type=F32)
    s_next = shift(state.astype(BF), FR, -1).astype(F32)
    earlier = earlier_frames(state.reshape(width, HD)).reshape(state.shape)
    me = lax.axis_index("y")
    flat = conv_weight.reshape(3 * width, NY * width)
    taps = []
    for away in range(NY):
        piece = lax.dynamic_slice_in_dim(flat, ((me + away) % NY) * width, width, 1)
        taps.append(lax.optimization_barrier(piece.T))
    here = earlier + state
    att = jnp.concatenate(
        [
            attend(q_prev, earlier.astype(BF)),
            attend(query, here.astype(BF)),
            attend(q_next, (here + s_next).astype(BF)),
        ],
        axis=0,
    )
    part = lambda away: jnp.dot(taps[away], att, preferred_element_type=F32)
    cut = (width // 2 + 15) // 16 * 16
    far = part(2).astype(BF)
    a_up = ring(far[:cut], "y", 1)
    a_down = ring(far[cut:], "y", -1)
    up = part(1)
    down = part(3)
    b_up = ring(up[cut:].astype(BF), "y", 1)
    b_down = ring(down[:cut].astype(BF), "y", -1)
    own = part(0)
    c_up = ring((up[:cut] + a_up.astype(F32)).astype(BF), "y", 1)
    c_down = ring((down[cut:] + a_down.astype(F32)).astype(BF), "y", -1)
    top = own[:cut] + c_up.astype(F32) + b_down.astype(F32)
    bottom = own[cut:] + b_up.astype(F32) + c_down.astype(F32)
    gate = jax.nn.silu(gate_act.T.astype(F32))
    out = jnp.concatenate([(top * gate[:cut]).astype(BF), (bottom * gate[cut:]).astype(BF)], axis=0)
    return out.T


def solution(mesh):
    fine = Mesh(mesh.devices.reshape(NZ, NX, NC, NY), FR + ("y",))
    act = P(FR, "y")
    return jax.shard_map(
        shards,
        mesh=fine,
        in_specs=(act, act, act, P(None, "y", None), act),
        out_specs=act,
        check_vma=False,
    )
```

```python
import jax
import jax.numpy as jnp
from jax import lax
from jax.sharding import Mesh, PartitionSpec as P


HD = 112
TPF = 880
BF = jnp.bfloat16
F32 = jnp.float32
NZ, NX, NC, NY = 8, 4, 2, 4
FR = ("z", "x", "c")


def ring(value, axis, step):
    count = lax.axis_size(axis)
    return lax.ppermute(value, axis, [(i, (i + step) % count) for i in range(count)])


def after(value, anchor):
    return lax.optimization_barrier((value, anchor))[0]


def earlier_frames(state, slice_weights):
    half = state.shape[0] // 2
    core = lax.axis_index("c")
    x_at = lax.axis_index("x")
    mine = lax.dynamic_slice_in_dim(state, core * half, half, 0)
    other = lax.dynamic_slice_in_dim(state, (1 - core) * half, half, 0)
    theirs = ring(other.astype(BF), "c", 1).astype(F32)
    chip = mine + theirs
    chip_bf = chip.astype(BF)
    total, before = chip, jnp.zeros_like(chip)
    for step in (1, 2, 3):
        got = ring(chip_bf, "x", step).astype(F32)
        total = total + got
        before = before + jnp.where(x_at >= step, got, 0.0)
    total_bf = total.astype(BF)
    taps = {2: slice_weights(2, chip_bf), 1: slice_weights(1, total_bf)}
    z_at = lax.axis_index("z")
    last = lax.axis_size("z") - 1
    below = jnp.where(z_at >= 1, ring(total_bf, "z", 1).astype(F32), 0.0)
    above = ring(total_bf, "z", -1).astype(F32)
    for_up = (above + jnp.where(z_at == last, 0.0, total + below)).astype(BF)
    for_down = (total + below).astype(BF)
    taps[3] = slice_weights(3, for_up)
    from_below = jnp.where(z_at >= 2, ring(for_up, "z", 3).astype(F32), 0.0)
    from_above = jnp.where(z_at >= 5, ring(for_down, "z", -3).astype(F32), 0.0)
    before = before + (below + jnp.where(z_at == last, above, 0.0) + (from_below + from_above))
    to_other = jnp.where(core == 0, before + mine, before)
    to_self = jnp.where(core == 0, before, before + theirs)
    from_other = ring(to_other.astype(BF), "c", 1).astype(F32)
    first = jnp.where(core == 0, to_self, from_other)
    second = jnp.where(core == 0, from_other, to_self)
    return jnp.concatenate([first, second], axis=0), taps


def attend(query, prefix):
    readout = jnp.einsum("hab,hat->hbt", prefix, jnp.maximum(query, 0), preferred_element_type=F32)
    scale = lax.rsqrt(jnp.mean(readout * readout, axis=1, keepdims=True) + 1e-06)
    return (readout * scale).astype(BF).reshape(-1, query.shape[-1])


def shards(query_act, key_act, value_act, conv_weight, gate_act):
    heads = query_act.shape[1] // HD
    width = heads * HD
    turned = lambda a: a.T.reshape(heads, HD, TPF)
    query = turned(query_act)
    q_prev = ring(query, FR, 1)
    q_next = ring(query, FR, -1)
    key = jnp.maximum(turned(key_act), 0)
    state = jnp.einsum("hat,hbt->hab", key, turned(value_act), preferred_element_type=F32)
    s_next = ring(state.astype(BF), FR, -1).astype(F32)
    me = lax.axis_index("y")
    frame, frames = lax.axis_index(FR), lax.axis_size(FR)
    flat = conv_weight.reshape(3 * width, NY * width)

    def slice_weights(away, anchor):
        return lax.dynamic_slice_in_dim(flat, ((me + away) % NY) * width, width, 1)

    earlier, taps = earlier_frames(state.reshape(width, HD), slice_weights)
    earlier = earlier.reshape(state.shape)
    here = earlier + state
    own_att = attend(query, here.astype(BF))
    att = jnp.concatenate(
        [
            attend(q_prev, earlier.astype(BF)),
            own_att,
            attend(q_next, jnp.where(frame < frames - 1, here + s_next, 0.0).astype(BF)),
        ],
        axis=0,
    )

    def part(away, dtype):
        weights = taps[away] if away in taps else slice_weights(away, far)
        return lax.dot_general(weights, att, (((0,), (0,)), ((), ())), preferred_element_type=F32).astype(dtype)

    cut = (width // 2 + 15) // 16 * 16
    far = part(2, BF)
    a_up = ring(far[:cut], "y", 1)
    a_down = ring(far[cut:], "y", -1)
    up = part(1, F32)
    down = part(3, F32)
    b_up = ring(up[cut:].astype(BF), "y", 1)
    b_down = ring(down[:cut].astype(BF), "y", -1)
    own = part(0, F32)
    c_up = ring((up[:cut] + a_up.astype(F32)).astype(BF), "y", 1)
    c_down = ring((down[cut:] + a_down.astype(F32)).astype(BF), "y", -1)
    gate = jax.nn.silu(after(gate_act, far).T.astype(F32))
    top = own[:cut] + c_up.astype(F32) + b_down.astype(F32)
    bottom = own[cut:] + b_up.astype(F32) + c_down.astype(F32)
    out = jnp.concatenate([(top * gate[:cut]).astype(BF), (bottom * gate[cut:]).astype(BF)], axis=0)
    return out.T


def solution(mesh):
    fine = Mesh(mesh.devices.reshape(NZ, NX, NC, NY), FR + ("y",))
    act = P(FR, "y")

    return jax.shard_map(
        shards,
        mesh=fine,
        in_specs=(act, act, act, P(None, "y", None), act),
        out_specs=act,
        check_vma=False,
    )
```
